32 devices in a mesh: integral: 4 (over x, core), pair: 8 (over z, y).
Axes of the slice: x: 2, y: 2, z: 4, core: 2. Of those that a mesh axis runs over, the one named last changes fastest.
Arguments:
- t2_tiles: bfloat16 [1024, 20, 1024], P('pair', None, 'integral'), may hold values from -6 to 6
- keep_tile: int32 [20], replicated, may hold values from 0 to 31, as said below
- integrals: bfloat16 [32, 1024, 4096], P('pair', None, 'integral'), may hold values from -0.078125 to 0.078125
Outputs:
- residual: bfloat16 [1024, 4096], P('pair', 'integral')
The draws below stay inside these ranges and needn't reach their ends.
Inputs may be any that keep to these rules, and one draw needn't show every extreme that they name: `keep_tile`: 20 distinct tile numbers in no particular order; tile k lies in the integral rows of pair index k // 4; at least one pair index has all 4 of its tiles listed.
All inputs are finite; a program needn't handle non-finite values.
Results may differ from the reference program's by a relative error of at most 0.0014.
Values may be sent and summed in bfloat16 or wider, within the bound.
A program may use at most 128 MiB of HBM per device.

```python
import jax
import jax.numpy as jnp
from jax import lax

TT = 1024
KT_DEV = 4
KT = 32
NKEEP = 20
OPAIRS = 1024
QW = 4096


def draw_keep_tile(key, part):
    owner_total = KT // KT_DEV
    first_key, second_key, third_key = jax.random.split(key, 3)
    full_owner = jax.random.randint(first_key, (), 0, owner_total)
    tile_ids = jnp.arange(KT, dtype=jnp.int32)
    shuffled = jax.random.permutation(second_key, KT).astype(jnp.int32)
    scores = jnp.where(tile_ids // KT_DEV == full_owner, tile_ids - KT, shuffled)
    picked = jnp.argsort(scores, stable=True)[:NKEEP]
    return picked[jax.random.permutation(third_key, NKEEP)].astype(jnp.int32)


def level_of(stream_key, extent, pieces, low, largest):
    factor_of = 1.0
    for position, blocks in pieces:
        heights = jax.random.uniform(jax.random.fold_in(jax.random.fold_in(stream_key, 6), position), (blocks,), jnp.float32, low / len(pieces), largest / len(pieces))
        factor_of = factor_of * jnp.repeat(jnp.exp(heights), extent[position] // blocks).reshape((-1,) + (1,) * (len(extent) - 1 - position))
    return factor_of


def gaussian(own_key, shape, spread, most, cuts=(), held_as=jnp.bfloat16):
    entries = jax.random.normal(own_key, shape, jnp.float32) * spread
    if len(cuts) > 0:
        entries = level_of(own_key, shape, cuts, -0.22, 0.18) * entries
    return jnp.clip(entries, min=-most, max=most).astype(held_as)


def setup_inputs(seed: int = 0) -> dict:
    seeds = jax.random.split(jax.random.key(seed), 4)
    t2_tiles = gaussian(seeds[0], (OPAIRS, NKEEP, TT), 1.0, 6.0, ((0, 8), (2, 4)))
    keep_tile = draw_keep_tile(jax.random.fold_in(seeds[3], 71), 0)
    integrals = gaussian(seeds[2], (KT, TT, QW), (NKEEP * TT // 4) ** -0.5, 0.078125, ((0, 8), (2, 4)))
    return {"t2_tiles": t2_tiles, "keep_tile": keep_tile, "integrals": integrals}


def reference(t2_tiles, keep_tile, integrals):
    def add_tile(running, inputs):
        amp_rows, tile_number = inputs
        v_rows = lax.dynamic_index_in_dim(integrals, tile_number, 0, keepdims=False)
        return running + jnp.dot(amp_rows, v_rows, preferred_element_type=jnp.float32), None

    start_sum = jnp.zeros((t2_tiles.shape[0], integrals.shape[2]), jnp.float32)
    partial_value, _ = lax.scan(add_tile, start_sum, (jnp.swapaxes(t2_tiles, 0, 1), keep_tile.astype(jnp.int32)))
    return (0.5 * partial_value).astype(jnp.bfloat16)
```

```python
import functools

import jax
import jax.numpy as jnp
from jax import lax
from jax.experimental import pallas as pl
from jax.experimental.pallas import tpu as pltpu
from jax.sharding import PartitionSpec as P

MESH = pl.DeviceIdType.MESH
CORES = 2


def inner_of(count):
    return 2 ** ((count.bit_length() - 1) // 2)


def ladder_kernel(
    dims, idx_ref, t2_ref, v_ref, out_ref,
    packed, amps, ints, part, y_in, z_in,
    v_sem, own_sem, a_send, a_recv, x_send, x_recv, c_send, c_recv, y_send, y_recv, z_send, z_recv,
):
    np_, ny, ni, slots, rows, cols = dims
    nz, nx = np_ // ny, ni // CORES
    kept = t2_ref.shape[0]
    qw = v_ref.shape[2]
    p, i = lax.axis_index("pair"), lax.axis_index("integral")
    z, y = p // ny, p % ny
    x, c = i // CORES, i % CORES
    other = x * CORES + (1 - c)

    load_v = pltpu.make_async_copy(v_ref, ints, v_sem)
    load_v.start()

    barrier = pltpu.get_barrier_semaphore()
    for d in range(1, np_):
        pl.semaphore_signal(barrier, inc=1, device_id={"pair": (p + d) % np_}, device_id_type=MESH)
    for d in range(1, nx):
        pl.semaphore_signal(
            barrier, inc=1, device_id={"integral": ((x + d) % nx) * CORES + c}, device_id_type=MESH
        )
    pl.semaphore_signal(barrier, inc=1, device_id={"integral": other}, device_id_type=MESH)

    def pack(owner):
        for s in range(slots):
            at = idx_ref[owner * slots + s]
            tile = t2_ref[jnp.minimum(at, kept - 1)]
            packed[owner, s] = jnp.where(at < kept, tile, jnp.zeros_like(tile))

    def block(source, part_i):
        return amps.at[:, pl.ds(pl.multiple_of(source * rows, rows), rows), pl.ds(pl.multiple_of(part_i * cols, cols), cols)]

    def a_copy(dest, source):
        return pltpu.make_async_remote_copy(
            src_ref=packed.at[dest], dst_ref=block(source, i), send_sem=a_send.at[dest], recv_sem=a_recv.at[source],
            device_id={"pair": dest}, device_id_type=MESH,
        )

    def x_copy(source, dest_x, from_x):
        region = block(source, from_x * CORES + c)
        return pltpu.make_async_remote_copy(
            src_ref=region, dst_ref=region, send_sem=x_send.at[dest_x, source], recv_sem=x_recv.at[from_x, source],
            device_id={"integral": dest_x * CORES + c}, device_id_type=MESH,
        )

    def c_copy(source, part_x, part_c):
        region = block(source, part_x * CORES + part_c)
        return pltpu.make_async_remote_copy(
            src_ref=region, dst_ref=region, send_sem=c_send.at[part_x, source], recv_sem=c_recv.at[part_x, source],
            device_id={"integral": other}, device_id_type=MESH,
        )

    own_copy = pltpu.make_async_copy(packed.at[p], block(p, i), own_sem)

    def y_copy(zc, d):
        return pltpu.make_async_remote_copy(
            src_ref=part.at[zc, (y + d) % ny], dst_ref=y_in.at[d - 1, zc],
            send_sem=y_send.at[d - 1, zc], recv_sem=y_recv.at[d - 1, zc],
            device_id={"pair": z * ny + (y + d) % ny}, device_id_type=MESH,
        )

    def z_copy(k):
        zc = (z + nz - k) % nz
        return pltpu.make_async_remote_copy(
            src_ref=part.at[zc, y], dst_ref=z_in.at[k - 1],
            send_sem=z_send.at[k - 1], recv_sem=z_recv.at[k - 1],
            device_id={"pair": zc * ny + y}, device_id_type=MESH,
        )

    def send_order():
        for dz in range(nz):
            for dy in range(ny):
                yield dz, dy, ((z + dz) % nz) * ny + (y + dy) % ny

    first = True
    for dz, dy, dest in send_order():
        pack(dest)
        if dz == 0 and dy == 0:
            own_copy.start()
            continue
        if first:
            pl.semaphore_wait(barrier, np_ - 1 + nx - 1 + 1)
            first = False
        a_copy(dest, p).start()

    def sources(k):
        zc = (z + nz - k) % nz
        for dy in range(ny):
            yield dy, zc * ny + (y + ny - dy) % ny

    def spread(k):
        for dy, source in sources(k):
            if k == 0 and dy == 0:
                own_copy.wait()
            else:
                a_copy(p, source).wait_recv()
            for d in range(1, nx):
                x_copy(source, (x + d) % nx, x).start()
            c_copy(source, x, c).start()

    def forward(k):
        for dy, source in sources(k):
            for d in range(1, nx):
                from_x = (x + d) % nx
                x_copy(source, x, from_x).wait_recv()
                c_copy(source, from_x, c).start()

    def multiply(k):
        zc = (z + nz - k) % nz
        for dy, source in sources(k):
            for xx in range(nx):
                c_copy(source, xx, 1 - c).wait_recv()
        if k == 0:
            load_v.wait()
        span = ny * rows
        left = pl.ds(pl.multiple_of(zc * span, span), span)
        wide = 256

        @pl.loop(0, qw // wide)
        def _(n):
            right = pl.ds(pl.multiple_of(n * wide, wide), wide)
            total = jnp.zeros((span, wide), jnp.float32)
            for s in range(slots):
                total += jnp.dot(amps[s, left, :], ints[s, :, right], preferred_element_type=jnp.float32)
            part[zc, :, :, right] = total.reshape(ny, rows, wide)

        for d in range(1, ny):
            y_copy(zc, d).start()

    def reduce_y(k):
        zc = (z + nz - k) % nz
        for d in range(1, ny):
            y_copy(zc, d).wait_recv()
        total = part[zc, y]
        for d in range(1, ny):
            total += y_in[d - 1, zc]
        part[zc, y] = total
        if k > 0:
            z_copy(k).start()

    for t in range(nz + 3):
        if t < nz:
            spread(t)
        if 0 <= t - 1 < nz:
            forward(t - 1)
        if 0 <= t - 2 < nz:
            reduce_y(t - 2)
        if 0 <= t - 1 < nz:
            multiply(t - 1)

    total = part[z, y]
    for k in range(1, nz):
        z_copy(k).wait_recv()
        total += z_in[k - 1]
    out_ref[...] = (0.5 * total).astype(out_ref.dtype)

    for dz, dy, dest in send_order():
        if dz or dy:
            a_copy(dest, p).wait_send()
    for k in range(nz):
        zc = (z + nz - k) % nz
        for dy, source in sources(k):
            for d in range(1, nx):
                x_copy(source, (x + d) % nx, x).wait_send()
            for xx in range(nx):
                c_copy(source, xx, c).wait_send()
        for d in range(1, ny):
            y_copy(zc, d).wait_send()
        if k > 0:
            z_copy(k).wait_send()


def on_device(t2_tiles, keep_tile, integrals):
    np_, ni = lax.axis_size("pair"), lax.axis_size("integral")
    rows, kept, cols = t2_tiles.shape
    slots, tt, qw = integrals.shape
    ny = inner_of(np_)
    nz, nx = np_ // ny, ni // CORES
    tiles = jnp.arange(np_ * slots, dtype=jnp.int32)
    positions = jnp.arange(kept, dtype=jnp.int32)
    idx = kept + jnp.sum(jnp.where(keep_tile[None, :] == tiles[:, None], positions[None, :] - kept, 0), axis=1)
    by_tile = jnp.swapaxes(t2_tiles, 0, 1)
    dma = pltpu.SemaphoreType.DMA
    dims = (np_, ny, ni, slots, rows, cols)
    return pl.pallas_call(
        functools.partial(ladder_kernel, dims),
        out_shape=jax.ShapeDtypeStruct((rows, qw), jnp.bfloat16),
        in_specs=[
            pl.BlockSpec(memory_space=pltpu.SMEM),
            pl.BlockSpec(memory_space=pltpu.VMEM),
            pl.BlockSpec(memory_space=pl.ANY),
        ],
        out_specs=pl.BlockSpec(memory_space=pltpu.VMEM),
        scratch_shapes=[
            pltpu.VMEM((np_, slots, rows, cols), jnp.bfloat16),
            pltpu.VMEM((slots, np_ * rows, tt), jnp.bfloat16),
            pltpu.VMEM((slots, tt, qw), jnp.bfloat16),
            pltpu.VMEM((nz, ny, rows, qw), jnp.float32),
            pltpu.VMEM((ny - 1, nz, rows, qw), jnp.float32),
            pltpu.VMEM((nz - 1, rows, qw), jnp.float32),
            dma, dma,
            dma((np_,)), dma((np_,)),
            dma((nx, np_)), dma((nx, np_)),
            dma((nx, np_)), dma((nx, np_)),
            dma((ny - 1, nz)), dma((ny - 1, nz)),
            dma((nz - 1,)), dma((nz - 1,)),
        ],
        compiler_params=pltpu.CompilerParams(
            collective_id=0, has_side_effects=True, vmem_limit_bytes=60 * 1024 * 1024
        ),
    )(idx.astype(jnp.int32), by_tile, integrals)


def solution(mesh):
    placed = (P("pair", None, "integral"), P(), P("pair", None, "integral"))
    return jax.shard_map(
        on_device, mesh=mesh, in_specs=placed, out_specs=P("pair", "integral"), check_vma=False
    )
```

```python
import functools
import itertools

import jax
import jax.numpy as jnp
from jax import lax
from jax.experimental import pallas as pl
from jax.experimental.pallas import tpu as pltpu
from jax.sharding import PartitionSpec as P

MESH = pl.DeviceIdType.MESH
CORES = 2
HALVES = 2
CUTS = 2


def inner_of(count):
    return 2 ** ((count.bit_length() - 1) // 2)


def order_of(count, first):
    away = sorted((at for at in range(count) if at != first), key=lambda at: -abs(at - first))
    return [first] + away


def ladder_kernel(
    dims, idx_ref, t2_ref, v_ref, out_ref,
    packed, amps, ints, part, y_in, low_in, high_in,
    v_sem, own_sem, a_send, a_recv, x_send, x_recv, c_send, c_recv, y_send, y_recv, z_send, low_recv, high_recv,
):
    np_, ny, ni, slots, rows, cols = dims
    nz, nx = np_ // ny, ni // CORES
    piece = rows // CUTS
    kept = t2_ref.shape[0]
    qw = v_ref.shape[2]
    p, i = lax.axis_index("pair"), lax.axis_index("integral")
    z, y = p // ny, p % ny
    x, c = i // CORES, i % CORES
    other = x * CORES + (1 - c)
    tables = [order_of(nz, at) for at in range(nz)]
    order = [sum(jnp.where(z == at, tables[at][k], 0) for at in range(nz)) for k in range(nz)]

    load_v = pltpu.make_async_copy(v_ref, ints, v_sem)
    load_v.start()

    barrier = pltpu.get_barrier_semaphore()
    for d in range(1, np_):
        pl.semaphore_signal(barrier, inc=1, device_id={"pair": (p + d) % np_}, device_id_type=MESH)
    for d in range(1, nx):
        pl.semaphore_signal(
            barrier, inc=1, device_id={"integral": ((x + d) % nx) * CORES + c}, device_id_type=MESH
        )
    pl.semaphore_signal(barrier, inc=1, device_id={"integral": other}, device_id_type=MESH)

    def pack(owner, r):
        for s in range(slots):
            at = idx_ref[owner * slots + s]
            tile = t2_ref[jnp.minimum(at, kept - 1), r * piece : (r + 1) * piece, :]
            packed[owner, r, s] = jnp.where(at < kept, tile, jnp.zeros_like(tile))

    def block(source, r, part_i):
        start = (((source // ny) * CUTS + r) * ny + source % ny) * piece
        return amps.at[:, pl.ds(pl.multiple_of(start, piece), piece), pl.ds(pl.multiple_of(part_i * cols, cols), cols)]

    def a_copy(dest, source, r):
        return pltpu.make_async_remote_copy(
            src_ref=packed.at[dest, r], dst_ref=block(source, r, i),
            send_sem=a_send.at[dest, r], recv_sem=a_recv.at[source, r],
            device_id={"pair": dest}, device_id_type=MESH,
        )

    def x_copy(source, r, dest_x, from_x):
        region = block(source, r, from_x * CORES + c)
        return pltpu.make_async_remote_copy(
            src_ref=region, dst_ref=region, send_sem=x_send.at[dest_x, source, r], recv_sem=x_recv.at[from_x, source, r],
            device_id={"integral": dest_x * CORES + c}, device_id_type=MESH,
        )

    def c_copy(source, r, part_x, part_c):
        region = block(source, r, part_x * CORES + part_c)
        return pltpu.make_async_remote_copy(
            src_ref=region, dst_ref=region, send_sem=c_send.at[part_x, source, r], recv_sem=c_recv.at[part_x, source, r],
            device_id={"integral": other}, device_id_type=MESH,
        )

    def own_copy(r):
        return pltpu.make_async_copy(packed.at[p, r], block(p, r, i), own_sem.at[r])

    def y_copy(zc, r, d, h):
        return pltpu.make_async_remote_copy(
            src_ref=part.at[zc, r, (y + d) % ny, h], dst_ref=y_in.at[d - 1, zc, r, h],
            send_sem=y_send.at[d - 1, zc, r, h], recv_sem=y_recv.at[d - 1, zc, r, h],
            device_id={"pair": z * ny + (y + d) % ny}, device_id_type=MESH,
        )

    def up_copy(zc, r, h):
        return pltpu.make_async_remote_copy(
            src_ref=part.at[zc, r, y, h], dst_ref=low_in.at[zc, r, h],
            send_sem=z_send.at[zc, r, h], recv_sem=low_recv.at[zc, r, h],
            device_id={"pair": (p + ny) % np_}, device_id_type=MESH,
        )

    def down_copy(zc, r, h):
        return pltpu.make_async_remote_copy(
            src_ref=part.at[zc, r, y, h], dst_ref=high_in.at[zc, r, h],
            send_sem=z_send.at[zc, r, h], recv_sem=high_recv.at[zc, r, h],
            device_id={"pair": (p + np_ - ny) % np_}, device_id_type=MESH,
        )

    def send_order():
        for dz, r, dy in itertools.product(range(nz), range(CUTS), range(ny)):
            yield dz, r, dy, order[dz] * ny + (y + dy) % ny

    first = True
    for dz, r, dy, dest in send_order():
        pack(dest, r)
        if dz == 0 and dy == 0:
            own_copy(r).start()
            continue
        if first:
            pl.semaphore_wait(barrier, np_ - 1 + nx - 1 + 1)
            first = False
        a_copy(dest, p, r).start()

    def sources(k):
        zc = order[k]
        for dy in range(ny):
            yield dy, zc * ny + (y + ny - dy) % ny

    def spread(k, r):
        for dy, source in sources(k):
            if k == 0 and dy == 0:
                own_copy(r).wait()
            else:
                a_copy(p, source, r).wait_recv()
            for d in range(1, nx):
                x_copy(source, r, (x + d) % nx, x).start()
            c_copy(source, r, x, c).start()

    def forward(k, r):
        for dy, source in sources(k):
            for d in range(1, nx):
                from_x = (x + d) % nx
                x_copy(source, r, x, from_x).wait_recv()
                c_copy(source, r, from_x, c).start()

    def multiply(k, r):
        zc = order[k]
        for dy, source in sources(k):
            for xx in range(nx):
                c_copy(source, r, xx, 1 - c).wait_recv()
        if k == 0 and r == 0:
            load_v.wait()
        span = ny * piece
        left = pl.ds(pl.multiple_of((zc * CUTS + r) * span, span), span)
        wide = 256
        part_cols = qw // HALVES
        for h in range(HALVES):
            @pl.loop(0, part_cols // wide)
            def _(n):
                right = pl.ds(pl.multiple_of(h * part_cols + n * wide, wide), wide)
                into = pl.ds(pl.multiple_of(n * wide, wide), wide)
                total = jnp.zeros((span, wide), jnp.float32)
                for s in range(slots):
                    total += jnp.dot(amps[s, left, :], ints[s, :, right], preferred_element_type=jnp.float32)
                part[zc, r, :, h, :, into] = total.reshape(ny, piece, wide)

            for d in range(1, ny):
                y_copy(zc, r, d, h).start()

    def reduce_y(k, r):
        zc = order[k]
        for h in range(HALVES):
            for d in range(1, ny):
                y_copy(zc, r, d, h).wait_recv()
            total = part[zc, r, y, h]
            for d in range(1, ny):
                total += y_in[d - 1, zc, r, h]
            part[zc, r, y, h] = total
            if k > 0:
                @pl.when((z == 0) & (zc > z))
                def _():
                    up_copy(zc, r, h).start()

                @pl.when((z == nz - 1) & (zc < z))
                def _():
                    down_copy(zc, r, h).start()

    def reduce_z(k, r):
        zc = order[k]
        for h in range(HALVES):
            @pl.when((z > 0) & (zc > z))
            def _():
                up_copy(zc, r, h).wait_recv()
                part[zc, r, y, h] += low_in[zc, r, h]
                up_copy(zc, r, h).start()

            @pl.when((z < nz - 1) & (zc < z))
            def _():
                down_copy(zc, r, h).wait_recv()
                part[zc, r, y, h] += high_in[zc, r, h]
                down_copy(zc, r, h).start()

    steps = list(itertools.product(range(nz), range(CUTS)))
    for t in range(len(steps) + 3):
        if t < len(steps):
            spread(*steps[t])
        if 0 <= t - 1 < len(steps):
            forward(*steps[t - 1])
            multiply(*steps[t - 1])
        if 0 <= t - 2 < len(steps):
            reduce_y(*steps[t - 2])
        if CUTS <= t - 3 < len(steps):
            reduce_z(*steps[t - 3])

    width = qw // HALVES
    for r, h in itertools.product(range(CUTS), range(HALVES)):
        @pl.when(z > 0)
        def _():
            up_copy(z, r, h).wait_recv()
            part[z, r, y, h] += low_in[z, r, h]

        @pl.when(z < nz - 1)
        def _():
            down_copy(z, r, h).wait_recv()
            part[z, r, y, h] += high_in[z, r, h]

        out_ref[r * piece : (r + 1) * piece, h * width : (h + 1) * width] = (0.5 * part[z, r, y, h]).astype(out_ref.dtype)

    for dz, r, dy, dest in send_order():
        if dz or dy:
            a_copy(dest, p, r).wait_send()
    for k, r in steps:
        zc = order[k]
        for dy, source in sources(k):
            for d in range(1, nx):
                x_copy(source, r, (x + d) % nx, x).wait_send()
            for xx in range(nx):
                c_copy(source, r, xx, c).wait_send()
        for h in range(HALVES):
            for d in range(1, ny):
                y_copy(zc, r, d, h).wait_send()
            if k > 0:
                up_copy(zc, r, h).wait_send()


def on_device(t2_tiles, keep_tile, integrals):
    np_, ni = lax.axis_size("pair"), lax.axis_size("integral")
    rows, kept, cols = t2_tiles.shape
    slots, tt, qw = integrals.shape
    ny = inner_of(np_)
    nz, nx = np_ // ny, ni // CORES
    tiles = jnp.arange(np_ * slots, dtype=jnp.int32)
    positions = jnp.arange(kept, dtype=jnp.int32)
    idx = kept + jnp.sum(jnp.where(keep_tile[None, :] == tiles[:, None], positions[None, :] - kept, 0), axis=1)
    by_tile = jnp.swapaxes(t2_tiles, 0, 1)
    dma = pltpu.SemaphoreType.DMA
    piece = rows // CUTS
    dims = (np_, ny, ni, slots, rows, cols)
    return pl.pallas_call(
        functools.partial(ladder_kernel, dims),
        out_shape=jax.ShapeDtypeStruct((rows, qw), jnp.bfloat16),
        in_specs=[
            pl.BlockSpec(memory_space=pltpu.SMEM),
            pl.BlockSpec(memory_space=pltpu.VMEM),
            pl.BlockSpec(memory_space=pl.ANY),
        ],
        out_specs=pl.BlockSpec(memory_space=pltpu.VMEM),
        scratch_shapes=[
            pltpu.VMEM((np_, CUTS, slots, piece, cols), jnp.bfloat16),
            pltpu.VMEM((slots, np_ * rows, tt), jnp.bfloat16),
            pltpu.VMEM((slots, tt, qw), jnp.bfloat16),
            pltpu.VMEM((nz, CUTS, ny, HALVES, piece, qw // HALVES), jnp.float32),
            pltpu.VMEM((ny - 1, nz, CUTS, HALVES, piece, qw // HALVES), jnp.float32),
            pltpu.VMEM((nz, CUTS, HALVES, piece, qw // HALVES), jnp.float32),
            pltpu.VMEM((nz, CUTS, HALVES, piece, qw // HALVES), jnp.float32),
            dma, dma((CUTS,)),
            dma((np_, CUTS)), dma((np_, CUTS)),
            dma((nx, np_, CUTS)), dma((nx, np_, CUTS)),
            dma((nx, np_, CUTS)), dma((nx, np_, CUTS)),
            dma((ny - 1, nz, CUTS, HALVES)), dma((ny - 1, nz, CUTS, HALVES)),
            dma((nz, CUTS, HALVES)), dma((nz, CUTS, HALVES)), dma((nz, CUTS, HALVES)),
        ],
        compiler_params=pltpu.CompilerParams(
            collective_id=0, has_side_effects=True, vmem_limit_bytes=60 * 1024 * 1024
        ),
    )(idx.astype(jnp.int32), by_tile, integrals)


def solution(mesh):
    placed = (P("pair", None, "integral"), P(), P("pair", None, "integral"))
    return jax.shard_map(
        on_device, mesh=mesh, in_specs=placed, out_specs=P("pair", "integral"), check_vma=False
    )
```
